256 devices in a mesh: row: 16 (over x, z_lo, core), col: 16 (over y, z_hi).
Axes of the slice: x: 4, y: 4, z: 8 (z_hi: 4, z_lo: 2; z = z_hi * 2 + z_lo), core: 2. Of those that a mesh axis runs over, the one named last changes fastest.
Arguments:
- vectors: bfloat16 [2048, 1024], P(('row', 'col')), may hold values from -6 to 6
- block_values: bfloat16 [16, 16, 512, 4096], P('row', 'col'), may hold values from -0.09375 to 0.09375
- block_rows: int32 [16, 16, 512], P('row', 'col'), may hold values from 0 to 127, as said below
- block_cols: int32 [16, 16, 512], P('row', 'col'), may hold values from 0 to 127, as said below
- block_count: int32 [16, 16], P('row', 'col'), may hold values from 0 to 512, as said below
Outputs:
- product: float32 [2048, 1024], P(('row', 'col'))
The draws below stay inside these ranges and needn't reach their ends.
Inputs may be any that keep to these rules, and one draw needn't show every extreme that they name: `block_rows`: in each tile the live slots name distinct positions with gi >= gj and come first, sorted by block row and then block column; slots past the count hold in-range indices that are not part of the matrix. `block_cols`: same slots as block_rows. `block_count`: some tile fills all 512 slots in every draw.
All inputs are finite; a program needn't handle non-finite values.
Results may differ from the reference program's by a relative error of at most 0.0003.
Values may be sent and summed in bfloat16 or wider, within the bound.
No kernel may reach another device: no remote copies, remote signals or barrier semaphores. Data moves between devices by JAX's collectives and lax.ppermute only.
A program may use at most 64 MiB of HBM per device.

```python
import jax
import jax.numpy as jnp
from jax import lax

NV = 16
BS = 64
PB = 8
NBMAX = 512
GR = 16
GC = 16
NBLK = 2048
VMAX = 16356


def block_pattern(key):
    base_key = jax.random.fold_in(key, 7)
    seg_rows = GC * PB
    seg_cols = GR * PB
    positions = seg_rows * seg_cols
    tile_keys = jax.random.split(base_key, GR * GC)

    def one_tile(tile_key, index):
        tile_row = index // GC
        tile_col = index % GC
        spots = jnp.arange(positions, dtype=jnp.int32)
        local_rows = spots // seg_cols
        local_cols = spots % seg_cols
        global_row = tile_row * GC * PB + local_rows
        global_col = (local_cols // PB * GC + tile_col) * PB + local_cols % PB
        valid = global_row >= global_col
        valid_count = jnp.sum(valid.astype(jnp.int32))
        base = valid_count * NBMAX // VMAX
        score_key, fill_key = jax.random.split(tile_key)
        factor = jax.random.randint(fill_key, (), 12, 17)
        count = jnp.minimum(base, base * factor // 16)
        heavy = jnp.logical_and(tile_row == GR - 1, tile_col == 0)
        count = jnp.where(heavy, base, count).astype(jnp.int32)
        scores = jax.random.randint(score_key, (positions,), 0, 32768) * 32768 + spots
        scores = jnp.where(valid, scores, -1 - spots)
        _, chosen = lax.top_k(scores, NBMAX)
        chosen = chosen.astype(jnp.int32)
        slot_ids = jnp.arange(NBMAX, dtype=jnp.int32)
        sort_keys = jnp.where(slot_ids < count, chosen, positions + chosen)
        order = jnp.argsort(sort_keys, stable=True)
        chosen = chosen[order]
        return (chosen // seg_cols, chosen % seg_cols, count)
    rows_all, cols_all, counts = jax.vmap(one_tile)(tile_keys, jnp.arange(GR * GC, dtype=jnp.int32))
    return (rows_all.reshape(GR, GC, NBMAX), cols_all.reshape(GR, GC, NBMAX), counts.reshape(GR, GC))


def draw_block_rows(key, part):
    return block_pattern(key)[0]


def draw_block_cols(key, part):
    return block_pattern(key)[1]


def draw_block_count(key, part):
    return block_pattern(key)[2]


def shard_levels(key, shape, cuts, least, largest):
    def one(position, blocks):
        heights = jax.random.uniform(jax.random.fold_in(jax.random.fold_in(key, 6), position), (blocks,), jnp.float32, least / len(cuts), largest / len(cuts))
        return jnp.repeat(jnp.exp(heights), shape[position] // blocks).reshape((-1,) + (1,) * (len(shape) - position - 1))

    level = one(*cuts[0])
    for cut in cuts[1:]:
        level = level * one(*cut)
    return level


def normal_values(key, shape, deviation, reach, pieces=(), kind=jnp.bfloat16):
    result = deviation * jax.random.normal(key, shape, jnp.float32)
    if pieces:
        result = result * shard_levels(key, shape, pieces, -0.22, 0.18)
    return jnp.clip(result, -reach, reach).astype(kind)


def setup_inputs(seed: int = 0) -> dict:
    streams_of = jax.random.split(jax.random.key(seed), 6)
    return {
        "vectors": normal_values(streams_of[0], (NBLK, NV * BS), 1.0, 6.0, ((0, 256),)),
        "block_values": normal_values(streams_of[1], (GR, GC, NBMAX, BS * BS), (1.0 / BS), 0.09375, ((0, 16), (1, 16))),
        "block_rows": draw_block_rows(jax.random.fold_in(streams_of[5], 71), 0),
        "block_cols": draw_block_cols(jax.random.fold_in(streams_of[5], 71), 0),
        "block_count": draw_block_count(jax.random.fold_in(streams_of[5], 71), 0),
    }


def reference(vectors, block_values, block_rows, block_cols, block_count):
    def tile(total, index):
        tile_row = index // GC
        tile_col = index % GC
        matrices = block_values[tile_row, tile_col].reshape(NBMAX, BS, BS).astype(jnp.float32)
        local_rows = block_rows[tile_row, tile_col].astype(jnp.int32)
        local_cols = block_cols[tile_row, tile_col].astype(jnp.int32)
        global_row = (tile_row * GC * PB + local_rows).astype(jnp.int32)
        global_col = (((local_cols // PB) * GC + tile_col) * PB + local_cols % PB).astype(jnp.int32)
        live = jnp.arange(NBMAX, dtype=jnp.int32) < block_count[tile_row, tile_col]
        weight = jnp.where(live, jnp.where(global_row == global_col, 0.5, 1.0), 0.0).astype(jnp.float32)
        col_vectors = vectors[global_col].astype(jnp.float32).reshape(NBMAX, NV, BS)
        row_vectors = vectors[global_row].astype(jnp.float32).reshape(NBMAX, NV, BS)
        forward = jnp.einsum("nvk,nik->nvi", col_vectors, matrices, precision=lax.Precision.HIGHEST)
        backward = jnp.einsum("nvi,nik->nvk", row_vectors, matrices, precision=lax.Precision.HIGHEST)
        forward = (forward * weight[:, None, None]).reshape(NBMAX, NV * BS)
        backward = (backward * weight[:, None, None]).reshape(NBMAX, NV * BS)
        total = total.at[global_row].add(forward)
        total = total.at[global_col].add(backward)
        return total, None

    start = jnp.zeros((NBLK, NV * BS), jnp.float32)
    total, _ = lax.scan(tile, start, jnp.arange(GR * GC, dtype=jnp.int32))
    return total
```

```python
import jax
import jax.numpy as jnp
from jax import lax
from jax.experimental import pallas as pl
from jax.experimental.pallas import tpu as pltpu
from jax.sharding import PartitionSpec as P

NV = 16
BS = 64
NB = 128
SLOTS = 512
GROUP = 128
PAD = 33
PITCH = 17
UNROLL = 32


def relayout_kernel(v_ref, w_ref, f_ref):
    for t in range(32):
        x = v_ref[:, t * 128 : (t + 1) * 128].astype(jnp.float32)
        for h in range(GROUP // 8):
            f_ref[pl.ds(h * 8 * PAD + t, 8, stride=PAD), :] = x[h * 8 : (h + 1) * 8]
    for s in range(GROUP):
        w_ref[s * 32 : (s + 1) * 32] = f_ref[s * PAD : s * PAD + 32].astype(jnp.bfloat16)


def relayout(values):
    return pl.pallas_call(
        relayout_kernel,
        grid=(SLOTS // GROUP,),
        in_specs=[pl.BlockSpec((GROUP, BS * BS), lambda i: (i, 0))],
        out_specs=pl.BlockSpec((GROUP * 32, 128), lambda i: (i, 0)),
        out_shape=jax.ShapeDtypeStruct((SLOTS * 32, 128), jnp.bfloat16),
        scratch_shapes=[pltpu.VMEM((GROUP * PAD, 128), jnp.float32)],
        name="relayout",
    )(values)


def even_odd(n, dtype):
    i = lax.broadcasted_iota(jnp.int32, (n, n), 0)
    j = lax.broadcasted_iota(jnp.int32, (n, n), 1)
    k = j % 64
    return (i == (j - k) + 2 * (k % 32) + k // 32).astype(dtype)


def expand(x_ref, xs_ref, tmp, permutation):
    for b in range(NB // 16):
        for q in range(8):
            x = x_ref[b * 16 : (b + 1) * 16, q * 128 : (q + 1) * 128].astype(jnp.float32)
            y = pltpu.roll(x, 64, 1)
            for h in range(2):
                base = (b * 16 + h * 8) * PITCH + 2 * q
                tmp[pl.ds(base, 8, stride=PITCH), :] = x[h * 8 : (h + 1) * 8]
                tmp[pl.ds(base + 1, 8, stride=PITCH), :] = y[h * 8 : (h + 1) * 8]
    for b in range(NB):
        z = tmp[b * PITCH : b * PITCH + 16, 0:64].astype(jnp.bfloat16)
        if permutation is not None:
            z = jnp.dot(z, permutation, preferred_element_type=jnp.float32).astype(jnp.bfloat16)
        xs_ref[b * 16 : (b + 1) * 16, :] = z


def compress(acc_ref, out_ref):
    lane = lax.broadcasted_iota(jnp.int32, (8, 128), 1)
    for b in range(NB // 8):
        for q in range(8):
            base = b * 8 * PITCH + 2 * q
            low = acc_ref[pl.ds(base, 8, stride=PITCH), :]
            high = acc_ref[pl.ds(base + 1, 8, stride=PITCH), :]
            out_ref[b * 8 : (b + 1) * 8, q * 128 : (q + 1) * 128] = jnp.where(
                lane < 64, low, pltpu.roll(high, 64, 1)
            )


def blocks_kernel(
    rows_ref, cols_ref, place_ref, xr_ref, xc_ref, w_ref, of_ref, og_ref, xrs, xcs, accf, accg, tmp
):
    expand(xr_ref, xrs, tmp, even_odd(64, jnp.bfloat16))
    expand(xc_ref, xcs, tmp, None)
    accf[...] = jnp.zeros_like(accf)
    accg[...] = jnp.zeros_like(accg)
    count = place_ref[0]
    row_index = place_ref[1]
    col_index = place_ref[2]

    def step(j, carry):
        for u in range(UNROLL):
            s = j * UNROLL + u
            r = rows_ref[s]
            c = cols_ref[s]
            global_row = row_index * NB + r
            global_col = ((c >> 3) * 16 + col_index) * 8 + (c & 7)
            weight = jnp.where(s < count, jnp.where(global_row == global_col, 0.5, 1.0), 0.0)
            w = w_ref[pl.ds(pl.multiple_of(s * 32, 32), 32), :]
            b = jnp.concatenate([w[:, :64], w[:, 64:]], 0)
            xc = xcs[pl.ds(pl.multiple_of(c * 16, 16), 16), :]
            xr = xrs[pl.ds(pl.multiple_of(r * 16, 16), 16), :]
            f = lax.dot_general(
                xc, b, (((1,), (1,)), ((), ())), preferred_element_type=jnp.float32
            )
            g = jnp.dot(xr, b, preferred_element_type=jnp.float32)
            accf[pl.ds(r * PITCH, 16), 0:64] += f * weight
            accg[pl.ds(c * PITCH, 16), 0:64] += g * weight
        return carry

    lax.fori_loop(0, (count + UNROLL - 1) // UNROLL, step, 0)
    compress(accf, of_ref)
    compress(accg, og_ref)


def blocks(rows, cols, place, row_vectors, col_vectors, w):
    smem = pl.BlockSpec(memory_space=pltpu.SMEM)
    vmem = pl.BlockSpec(memory_space=pltpu.VMEM)
    return pl.pallas_call(
        blocks_kernel,
        in_specs=[smem] * 3 + [vmem] * 3,
        out_specs=[vmem] * 2,
        out_shape=[jax.ShapeDtypeStruct((NB, NV * BS), jnp.float32)] * 2,
        scratch_shapes=[pltpu.VMEM((NB * NV, BS), jnp.bfloat16)] * 2
        + [pltpu.VMEM((NB * PITCH, 128), jnp.float32)] * 3,
        name="blocks",
    )(rows, cols, place, row_vectors, col_vectors, w)


def finish_kernel(a_ref, b_ref, o_ref):
    back = even_odd(128, jnp.float32)
    a = a_ref[0]
    b = b_ref[0]
    for i in range(1, 16):
        a = a + a_ref[i]
        b = b + b_ref[i]
    for q in range(8):
        piece = slice(q * 128, (q + 1) * 128)
        o_ref[:, piece] = b[:, piece] + lax.dot_general(
            a[:, piece],
            back,
            (((1,), (1,)), ((), ())),
            preferred_element_type=jnp.float32,
            precision=lax.Precision.HIGHEST,
        )


def finish(a, b):
    vmem = pl.BlockSpec(memory_space=pltpu.VMEM)
    return pl.pallas_call(
        finish_kernel,
        in_specs=[vmem] * 2,
        out_specs=vmem,
        out_shape=jax.ShapeDtypeStruct((8, NV * BS), jnp.float32),
        name="finish",
    )(a, b)


def on_device(vectors, block_values, block_rows, block_cols, block_count):
    row_index = lax.axis_index("row")
    col_index = lax.axis_index("col")
    copies = jnp.broadcast_to(vectors[None], (16,) + vectors.shape)
    column_set = lax.all_to_all(copies, "row", 0, 0, tiled=True).reshape(NB, NV * BS)
    row_segment = lax.all_to_all(copies, "col", 0, 0, tiled=True).reshape(NB, NV * BS)
    w = relayout(block_values.reshape(SLOTS, BS * BS))
    place = jnp.stack([block_count.reshape(()), row_index, col_index])
    row_part, col_part = blocks(
        block_rows.reshape(SLOTS), block_cols.reshape(SLOTS), place, row_segment, column_set, w
    )
    mine_rows = lax.all_to_all(row_part.reshape(16, 8, NV * BS), "col", 0, 0, tiled=True)
    mine_cols = lax.all_to_all(col_part.reshape(16, 8, NV * BS), "row", 0, 0, tiled=True)
    return finish(mine_rows, mine_cols)


def solution(mesh):
    placed = (
        P(("row", "col"), None),
        P("row", "col", None, None),
        P("row", "col", None),
        P("row", "col", None),
        P("row", "col"),
    )
    return jax.shard_map(
        on_device, mesh=mesh, in_specs=placed, out_specs=P(("row", "col"), None), check_vma=False
    )
```

```python
import functools

import jax
import jax.numpy as jnp
from jax import lax
from jax.experimental import pallas as pl
from jax.experimental.pallas import tpu as pltpu
from jax.sharding import PartitionSpec as P

NV = 16
BS = 64
NB = 128
SLOTS = 512
GROUP = 128
PAD = 33
PITCH = 17
UNROLL = 32
ROW_BITS = (3, 2, 1, 0)
COL_BITS = (1, 0, 3, 2)


def relayout_kernel(v_ref, w_ref, f_ref):
    for t in range(32):
        x = v_ref[:, t * 128 : (t + 1) * 128].astype(jnp.float32)
        for h in range(GROUP // 8):
            f_ref[pl.ds(h * 8 * PAD + t, 8, stride=PAD), :] = x[h * 8 : (h + 1) * 8]
    for s in range(GROUP):
        w_ref[s * 32 : (s + 1) * 32] = f_ref[s * PAD : s * PAD + 32].astype(jnp.bfloat16)


def relayout(values):
    return pl.pallas_call(
        relayout_kernel,
        grid=(SLOTS // GROUP,),
        in_specs=[pl.BlockSpec((GROUP, BS * BS), lambda i: (i, 0))],
        out_specs=pl.BlockSpec((GROUP * 32, 128), lambda i: (i, 0)),
        out_shape=jax.ShapeDtypeStruct((SLOTS * 32, 128), jnp.bfloat16),
        scratch_shapes=[pltpu.VMEM((GROUP * PAD, 128), jnp.float32)],
        name="relayout",
    )(values)


def even_odd(n, dtype):
    i = lax.broadcasted_iota(jnp.int32, (n, n), 0)
    j = lax.broadcasted_iota(jnp.int32, (n, n), 1)
    k = j % 64
    return (i == (j - k) + 2 * (k % 32) + k // 32).astype(dtype)


def expand(x_ref, xs_ref, tmp, permutation):
    for b in range(NB // 16):
        for q in range(8):
            x = x_ref[b * 16 : (b + 1) * 16, q * 128 : (q + 1) * 128].astype(jnp.float32)
            y = pltpu.roll(x, 64, 1)
            for h in range(2):
                base = (b * 16 + h * 8) * PITCH + 2 * q
                tmp[pl.ds(base, 8, stride=PITCH), :] = x[h * 8 : (h + 1) * 8]
                tmp[pl.ds(base + 1, 8, stride=PITCH), :] = y[h * 8 : (h + 1) * 8]
    for b in range(NB):
        z = tmp[b * PITCH : b * PITCH + 16, 0:64].astype(jnp.bfloat16)
        if permutation is not None:
            z = jnp.dot(z, permutation, preferred_element_type=jnp.float32).astype(jnp.bfloat16)
        xs_ref[b * 16 : (b + 1) * 16, :] = z


def compress(acc_ref, out_ref, first):
    lane = lax.broadcasted_iota(jnp.int32, (8, 128), 1)
    for b in range(out_ref.shape[0] // 8):
        for q in range(8):
            base = (first + b * 8) * PITCH + 2 * q
            low = acc_ref[pl.ds(base, 8, stride=PITCH), :]
            high = acc_ref[pl.ds(base + 1, 8, stride=PITCH), :]
            out_ref[b * 8 : (b + 1) * 8, q * 128 : (q + 1) * 128] = jnp.where(
                lane < 64, low, pltpu.roll(high, 64, 1)
            )


def product_kernel(
    backward, rows_ref, cols_ref, place_ref, x_ref, w_ref, keep_ref, send_ref, xs, acc, tmp
):
    expand(x_ref, xs, tmp, even_odd(64, jnp.bfloat16) if backward else None)
    acc[...] = jnp.zeros_like(acc)
    count = place_ref[0]
    row_index = place_ref[1]
    col_index = place_ref[2]
    contract = ((1,), (0,)) if backward else ((1,), (1,))

    def step(j, carry):
        for u in range(UNROLL):
            s = j * UNROLL + u
            r = rows_ref[s]
            c = cols_ref[s]
            global_row = row_index * NB + r
            global_col = ((c >> 3) * 16 + col_index) * 8 + (c & 7)
            weight = jnp.where(s < count, jnp.where(global_row == global_col, 0.5, 1.0), 0.0)
            r = place_ref[3 + (r >> 3)] + (r & 7)
            c = place_ref[19 + (c >> 3)] + (c & 7)
            source, target = (r, c) if backward else (c, r)
            w = w_ref[pl.ds(pl.multiple_of(s * 32, 32), 32), :]
            b = jnp.concatenate([w[:, :64], w[:, 64:]], 0)
            x = xs[pl.ds(pl.multiple_of(source * 16, 16), 16), :]
            f = lax.dot_general(x, b, (contract, ((), ())), preferred_element_type=jnp.float32)
            acc[pl.ds(target * PITCH, 16), 0:64] += f * weight
        return carry

    lax.fori_loop(0, (count + UNROLL - 1) // UNROLL, step, 0)
    compress(acc, keep_ref, 0)
    compress(acc, send_ref, NB // 2)


def product(backward, rows, cols, place, x, w):
    smem = pl.BlockSpec(memory_space=pltpu.SMEM)
    vmem = pl.BlockSpec(memory_space=pltpu.VMEM)
    return pl.pallas_call(
        functools.partial(product_kernel, backward),
        in_specs=[smem] * 3 + [vmem] * 2,
        out_specs=[vmem] * 2,
        out_shape=[jax.ShapeDtypeStruct((NB // 2, NV * BS), jnp.float32)] * 2,
        scratch_shapes=[pltpu.VMEM((NB * NV, BS), jnp.bfloat16)]
        + [pltpu.VMEM((NB * PITCH, 128), jnp.float32)] * 2,
        name="backward" if backward else "forward",
    )(rows, cols, place, x, w)


def finish_kernel(a0_ref, a1_ref, b0_ref, b1_ref, o_ref):
    back = even_odd(128, jnp.float32)
    for q in range(8):
        piece = slice(q * 128, (q + 1) * 128)
        a = a0_ref[:, piece] + a1_ref[:, piece]
        o_ref[:, piece] = (b0_ref[:, piece] + b1_ref[:, piece]) + lax.dot_general(
            a,
            back,
            (((1,), (1,)), ((), ())),
            preferred_element_type=jnp.float32,
            precision=lax.Precision.HIGHEST,
        )


def finish(a, b):
    vmem = pl.BlockSpec(memory_space=pltpu.VMEM)
    return pl.pallas_call(
        finish_kernel,
        in_specs=[vmem] * 4,
        out_specs=vmem,
        out_shape=jax.ShapeDtypeStruct((8, NV * BS), jnp.float32),
        name="finish",
    )(*a, *b)


def swap(x, axis, bit):
    return lax.ppermute(x, axis, [(s, s ^ (1 << bit)) for s in range(16)])


def gather(x, axis, bits):
    for bit in bits:
        x = jnp.concatenate([x, swap(x, axis, bit)], 0)
    return x


def scatter(keep, send, axis, bits):
    for k in reversed(range(4)):
        received = swap(send, axis, bits[k])
        if k == 0:
            return keep, received
        half = keep.shape[0] // 2
        keep, send = keep[:half] + received[:half], keep[half:] + received[half:]


def slots(me, bits):
    m = jnp.arange(16, dtype=jnp.int32) ^ me
    return sum(((m >> bit) & 1) << (k + 3) for k, bit in enumerate(bits))


def on_device(vectors, block_values, block_rows, block_cols, block_count):
    row_index = lax.axis_index("row")
    col_index = lax.axis_index("col")
    column_set = gather(vectors, "row", ROW_BITS)
    row_segment = gather(vectors, "col", COL_BITS)
    w = relayout(block_values.reshape(SLOTS, BS * BS))
    place = jnp.concatenate(
        [
            jnp.stack([block_count.reshape(()), row_index, col_index]),
            slots(col_index, COL_BITS),
            slots(row_index, ROW_BITS),
        ]
    )
    rows = block_rows.reshape(SLOTS)
    cols = block_cols.reshape(SLOTS)
    row_part = product(False, rows, cols, place, column_set, w)
    col_part = product(True, rows, cols, place, row_segment, w)
    mine_rows = scatter(*row_part, "col", COL_BITS)
    mine_cols = scatter(*col_part, "row", ROW_BITS)
    return finish(mine_rows, mine_cols)


def solution(mesh):
    placed = (
        P(("row", "col"), None),
        P("row", "col", None, None),
        P("row", "col", None),
        P("row", "col", None),
        P("row", "col"),
    )
    return jax.shard_map(
        on_device, mesh=mesh, in_specs=placed, out_specs=P(("row", "col"), None), check_vma=False
    )
```

```python
import functools

import jax
import jax.numpy as jnp
from jax import lax
from jax.experimental import pallas as pl
from jax.experimental.pallas import tpu as pltpu
from jax.sharding import PartitionSpec as P

NV = 16
BS = 64
NB = 128
SLOTS = 512
GROUP = 128
PAD = 33
UNROLL = 64
ROW_BITS = (3, 2, 1, 0)
COL_BITS = (1, 0, 3, 2)
MIB = 1 << 20


def relayout_kernel(v_ref, weight_ref, w_ref, f_ref):
    weight = weight_ref[...]
    for t in range(32):
        x = v_ref[:, t * 128 : (t + 1) * 128].astype(jnp.float32) * weight
        for h in range(GROUP // 8):
            f_ref[pl.ds(h * 8 * PAD + t, 8, stride=PAD), :] = x[h * 8 : (h + 1) * 8]
    for s in range(GROUP):
        w_ref[s * 32 : (s + 1) * 32] = f_ref[s * PAD : s * PAD + 32].astype(jnp.bfloat16)


def relayout(values, weight):
    return pl.pallas_call(
        relayout_kernel,
        grid=(SLOTS // GROUP,),
        in_specs=[
            pl.BlockSpec((GROUP, BS * BS), lambda i: (i, 0)),
            pl.BlockSpec((GROUP, 128), lambda i: (i, 0)),
        ],
        out_specs=pl.BlockSpec((GROUP * 32, 128), lambda i: (i, 0)),
        out_shape=jax.ShapeDtypeStruct((SLOTS * 32, 128), jnp.bfloat16),
        scratch_shapes=[pltpu.VMEM((GROUP * PAD, 128), jnp.float32)],
        compiler_params=pltpu.CompilerParams(vmem_limit_bytes=16 * MIB),
        name="relayout",
    )(values, weight)


def even_odd(dtype):
    i = lax.broadcasted_iota(jnp.int32, (128, 128), 0)
    j = lax.broadcasted_iota(jnp.int32, (128, 128), 1)
    k = j % 64
    return (i == (j - k) + 2 * (k % 32) + k // 32).astype(dtype)


def below(shape):
    return lax.broadcasted_iota(jnp.int32, shape, 1) < 64


def offset(ref, s):
    return pl.ds(pl.multiple_of(ref[s], 16), 16)


def pair_of_blocks(w_ref, s):
    w = w_ref[pl.ds(pl.multiple_of(s * 32, 64), 64), :]
    a, b = w[:32], w[32:]
    low = below((32, 128))
    return jnp.concatenate(
        [
            jnp.where(low, a, pltpu.roll(b, 64, 1)),
            jnp.where(low, pltpu.roll(a, 64, 1), b),
        ],
        0,
    )


def forward_kernel(count_ref, rows_ref, cols_ref, x_ref, w_ref, keep_ref, send_ref, xlo, xhi, acc):
    low = below((16, 128))
    for b in range(NB // 2):
        x = x_ref[b * 16 : (b + 1) * 16, :].astype(jnp.float32)
        y = pltpu.roll(x, 64, 1)
        for h in range(2):
            here = slice((2 * b + h) * 16, (2 * b + h + 1) * 16)
            p, q = x[h * 8 : (h + 1) * 8], y[h * 8 : (h + 1) * 8]
            zero = jnp.zeros((16, 128), jnp.float32)
            xlo[here, :] = jnp.where(low, jnp.concatenate([p, q], 0), zero).astype(jnp.bfloat16)
            xhi[here, :] = jnp.where(low, zero, jnp.concatenate([q, p], 0)).astype(jnp.bfloat16)
    acc[...] = jnp.zeros_like(acc)

    def step(j, carry):
        for u in range(0, UNROLL, 2):
            s = j * UNROLL + u
            b = pair_of_blocks(w_ref, s)
            x = jnp.concatenate([xlo[offset(cols_ref, s), :], xhi[offset(cols_ref, s + 1), :]], 0)
            f = lax.dot_general(
                x, b, (((1,), (1,)), ((), ())), preferred_element_type=jnp.float32
            )
            acc[offset(rows_ref, s), 0:64] += f[:16]
            acc[offset(rows_ref, s + 1), 0:64] += f[16:]
        return carry

    lax.fori_loop(0, (count_ref[0, 0] + UNROLL - 1) // UNROLL, step, 0)
    low = below((8, 128))
    for b in range(NB):
        a0, a1 = acc[b * 16 : b * 16 + 8, :], acc[b * 16 + 8 : b * 16 + 16, :]
        out, i = (keep_ref, b) if b < NB // 2 else (send_ref, b - NB // 2)
        out[i * 8 : (i + 1) * 8, :] = jnp.where(low, a0, pltpu.roll(a1, 64, 1))


def backward_kernel(count_ref, rows_ref, cols_ref, x_ref, w_ref, keep_ref, send_ref, xs, acc):
    order = even_odd(jnp.bfloat16)
    for b in range(NB // 8):
        x = jnp.dot(
            x_ref[b * 64 : (b + 1) * 64, :], order, preferred_element_type=jnp.float32
        )
        y = pltpu.roll(x, 64, 1)
        for h in range(8):
            here = slice((8 * b + h) * 16, (8 * b + h + 1) * 16)
            p, q = x[h * 8 : (h + 1) * 8], y[h * 8 : (h + 1) * 8]
            xs[here, :] = jnp.concatenate([p, q], 0).astype(jnp.bfloat16)
    acc[...] = jnp.zeros_like(acc)

    def step(j, carry):
        for u in range(0, UNROLL, 2):
            s = j * UNROLL + u
            b = pair_of_blocks(w_ref, s)
            x = jnp.concatenate(
                [xs[offset(rows_ref, s), 0:64], xs[offset(rows_ref, s + 1), 0:64]], 0
            )
            g = jnp.dot(x, b, preferred_element_type=jnp.float32)
            acc[offset(cols_ref, s), 0:64] += g[:16, 0:64]
            acc[offset(cols_ref, s + 1), 64:128] += g[16:, 64:128]
        return carry

    lax.fori_loop(0, (count_ref[0, 0] + UNROLL - 1) // UNROLL, step, 0)
    low = below((8, 128))
    for b in range(NB):
        a0, a1 = acc[b * 16 : b * 16 + 8, :], acc[b * 16 + 8 : b * 16 + 16, :]
        out, i = (keep_ref, b) if b < NB // 2 else (send_ref, b - NB // 2)
        out[i * 8 : (i + 1) * 8, :] = jnp.where(
            low, a0 + pltpu.roll(a0, 64, 1), a1 + pltpu.roll(a1, 64, 1)
        )


def product(backward, count, rows, cols, x, w):
    smem = pl.BlockSpec(memory_space=pltpu.SMEM)
    vmem = pl.BlockSpec(memory_space=pltpu.VMEM)
    tables = 1 if backward else 2
    return pl.pallas_call(
        backward_kernel if backward else forward_kernel,
        in_specs=[smem] * 3 + [vmem] * 2,
        out_specs=[vmem] * 2,
        out_shape=[jax.ShapeDtypeStruct((NB * 4, 128), jnp.float32)] * 2,
        scratch_shapes=[pltpu.VMEM((NB * NV, 128), jnp.bfloat16)] * tables
        + [pltpu.VMEM((NB * NV, 128), jnp.float32)],
        compiler_params=pltpu.CompilerParams(vmem_limit_bytes=16 * MIB),
        name="backward" if backward else "forward",
    )(count, rows, cols, x, w)


def finish_kernel(a0_ref, a1_ref, b0_ref, b1_ref, o_ref, tmp):
    back = even_odd(jnp.float32)
    tmp[...] = (b0_ref[...] + b1_ref[...]) + lax.dot_general(
        a0_ref[...] + a1_ref[...],
        back,
        (((1,), (1,)), ((), ())),
        preferred_element_type=jnp.float32,
        precision=lax.Precision.HIGHEST,
    )
    for q in range(8):
        o_ref[:, q * 128 : (q + 1) * 128] = tmp[pl.ds(q, 8, stride=8), :]


def finish(a, b):
    vmem = pl.BlockSpec(memory_space=pltpu.VMEM)
    return pl.pallas_call(
        finish_kernel,
        in_specs=[vmem] * 4,
        out_specs=vmem,
        out_shape=jax.ShapeDtypeStruct((8, NV * BS), jnp.float32),
        scratch_shapes=[pltpu.VMEM((64, 128), jnp.float32)],
        compiler_params=pltpu.CompilerParams(vmem_limit_bytes=4 * MIB),
        name="finish",
    )(*a, *b)


def swap(x, axis, bit):
    return lax.ppermute(x, axis, [(s, s ^ (1 << bit)) for s in range(16)])


def gather(x, axis, bits):
    for bit in bits:
        x = jnp.concatenate([x, swap(x, axis, bit)], 0)
    return x


def scatter(keep, send, axis, bits):
    for k in reversed(range(4)):
        received = swap(send, axis, bits[k])
        if k == 0:
            return keep, received
        half = keep.shape[0] // 2
        keep, send = keep[:half] + received[:half], keep[half:] + received[half:]


def place(position, me, bits):
    m = (position >> 3) ^ me
    slot = sum(((m >> bit) & 1) << k for k, bit in enumerate(bits))
    return (slot * 8 + (position & 7)) * 16


def on_device(vectors, block_values, block_rows, block_cols, block_count):
    row_index = lax.axis_index("row")
    col_index = lax.axis_index("col")
    piece = vectors.reshape(64, 128)
    column_set = gather(piece, "row", ROW_BITS)
    row_segment = gather(piece, "col", COL_BITS)
    local_rows = block_rows.reshape(SLOTS)
    local_cols = block_cols.reshape(SLOTS)
    global_row = row_index * NB + local_rows
    global_col = ((local_cols >> 3) * 16 + col_index) * 8 + (local_cols & 7)
    live = jnp.arange(SLOTS, dtype=jnp.int32) < block_count.reshape(())
    weight = jnp.where(live, jnp.where(global_row == global_col, 0.5, 1.0), 0.0)
    weight = jnp.broadcast_to(weight.astype(jnp.float32)[:, None], (SLOTS, 128))
    w = relayout(block_values.reshape(SLOTS, BS * BS), weight)
    rows = place(local_rows, col_index, COL_BITS)
    cols = place(local_cols, row_index, ROW_BITS)
    row_part = product(False, block_count, rows, cols, column_set, w)
    col_part = product(True, block_count, rows, cols, row_segment, w)
    mine_rows = scatter(*row_part, "col", COL_BITS)
    mine_cols = scatter(*col_part, "row", ROW_BITS)
    return finish(mine_rows, mine_cols)


def solution(mesh):
    placed = (
        P(("row", "col"), None),
        P("row", "col", None, None),
        P("row", "col", None),
        P("row", "col", None),
        P("row", "col"),
    )
    return jax.shard_map(
        on_device, mesh=mesh, in_specs=placed, out_specs=P(("row", "col"), None), check_vma=False
    )
```

```python
import functools

import jax
import jax.numpy as jnp
from jax import lax
from jax.experimental import pallas as pl
from jax.experimental.pallas import tpu as pltpu
from jax.sharding import PartitionSpec as P

NV = 16
BS = 64
NB = 128
SLOTS = 512
GROUP = 128
PAD = 33
UNROLL = 64
ROW_BITS = (3, 2, 1, 0)
COL_BITS = (1, 0, 3, 2)
MIB = 1 << 20
MODE = "rd"
BAR = "brf"


def relayout_kernel(v_ref, weight_ref, w_ref, f_ref):
    weight = weight_ref[...]
    for t in range(32):
        x = v_ref[:, t * 128 : (t + 1) * 128].astype(jnp.float32) * weight
        for h in range(GROUP // 8):
            f_ref[pl.ds(h * 8 * PAD + t, 8, stride=PAD), :] = x[h * 8 : (h + 1) * 8]
    for s in range(GROUP):
        w_ref[s * 32 : (s + 1) * 32] = f_ref[s * PAD : s * PAD + 32].astype(jnp.bfloat16)


def relayout(values, weight):
    return pl.pallas_call(
        relayout_kernel,
        grid=(SLOTS // GROUP,),
        in_specs=[
            pl.BlockSpec((GROUP, BS * BS), lambda i: (i, 0)),
            pl.BlockSpec((GROUP, 128), lambda i: (i, 0)),
        ],
        out_specs=pl.BlockSpec((GROUP * 32, 128), lambda i: (i, 0)),
        out_shape=jax.ShapeDtypeStruct((SLOTS * 32, 128), jnp.bfloat16),
        scratch_shapes=[pltpu.VMEM((GROUP * PAD, 128), jnp.float32)],
        compiler_params=pltpu.CompilerParams(vmem_limit_bytes=16 * MIB),
        name="relayout",
    )(values, weight)


def even_odd(dtype):
    i = lax.broadcasted_iota(jnp.int32, (128, 128), 0)
    j = lax.broadcasted_iota(jnp.int32, (128, 128), 1)
    k = j % 64
    return (i == (j - k) + 2 * (k % 32) + k // 32).astype(dtype)


def below(shape):
    return lax.broadcasted_iota(jnp.int32, shape, 1) < 64


def offset(ref, s):
    return pl.ds(pl.multiple_of(ref[s], 16), 16)


def pair_of_blocks(w_ref, s):
    w = w_ref[pl.ds(pl.multiple_of(s * 32, 64), 64), :]
    a, b = w[:32], w[32:]
    low = below((32, 128))
    return jnp.concatenate(
        [
            jnp.where(low, a, pltpu.roll(b, 64, 1)),
            jnp.where(low, pltpu.roll(a, 64, 1), b),
        ],
        0,
    )


def forward_kernel(count_ref, rows_ref, cols_ref, x_ref, w_ref, *outs_and_scratch):
    *outs, xlo, xhi, acc = outs_and_scratch
    low = below((16, 128))
    for b in range(NB // 2):
        x = x_ref[b * 16 : (b + 1) * 16, :].astype(jnp.float32)
        y = pltpu.roll(x, 64, 1)
        for h in range(2):
            here = slice((2 * b + h) * 16, (2 * b + h + 1) * 16)
            p, q = x[h * 8 : (h + 1) * 8], y[h * 8 : (h + 1) * 8]
            zero = jnp.zeros((16, 128), jnp.float32)
            xlo[here, :] = jnp.where(low, jnp.concatenate([p, q], 0), zero).astype(jnp.bfloat16)
            xhi[here, :] = jnp.where(low, zero, jnp.concatenate([q, p], 0)).astype(jnp.bfloat16)
    acc[...] = jnp.zeros_like(acc)

    def step(j, carry):
        for u in range(0, UNROLL, 2):
            s = j * UNROLL + u
            b = pair_of_blocks(w_ref, s)
            x = jnp.concatenate([xlo[offset(cols_ref, s), :], xhi[offset(cols_ref, s + 1), :]], 0)
            f = lax.dot_general(
                x, b, (((1,), (1,)), ((), ())), preferred_element_type=jnp.float32
            )
            acc[offset(rows_ref, s), 0:64] += f[:16]
            acc[offset(rows_ref, s + 1), 0:64] += f[16:]
        return carry

    lax.fori_loop(0, (count_ref[0, 0] + UNROLL - 1) // UNROLL, step, 0)
    low = below((8, 128))
    for b in range(NB):
        a0, a1 = acc[b * 16 : b * 16 + 8, :], acc[b * 16 + 8 : b * 16 + 16, :]
        out, i = outs[b * len(outs) // NB], b % (NB // len(outs))
        out[i * 8 : (i + 1) * 8, :] = jnp.where(low, a0, pltpu.roll(a1, 64, 1))


def backward_kernel(count_ref, rows_ref, cols_ref, x_ref, w_ref, *outs_and_scratch):
    *outs, xs, acc = outs_and_scratch
    order = even_odd(jnp.bfloat16)
    for b in range(NB // 8):
        x = jnp.dot(
            x_ref[b * 64 : (b + 1) * 64, :], order, preferred_element_type=jnp.float32
        )
        y = pltpu.roll(x, 64, 1)
        for h in range(8):
            here = slice((8 * b + h) * 16, (8 * b + h + 1) * 16)
            p, q = x[h * 8 : (h + 1) * 8], y[h * 8 : (h + 1) * 8]
            xs[here, :] = jnp.concatenate([p, q], 0).astype(jnp.bfloat16)
    acc[...] = jnp.zeros_like(acc)

    def step(j, carry):
        for u in range(0, UNROLL, 2):
            s = j * UNROLL + u
            b = pair_of_blocks(w_ref, s)
            x = jnp.concatenate(
                [xs[offset(rows_ref, s), 0:64], xs[offset(rows_ref, s + 1), 0:64]], 0
            )
            g = jnp.dot(x, b, preferred_element_type=jnp.float32)
            acc[offset(cols_ref, s), 0:64] += g[:16, 0:64]
            acc[offset(cols_ref, s + 1), 64:128] += g[16:, 64:128]
        return carry

    lax.fori_loop(0, (count_ref[0, 0] + UNROLL - 1) // UNROLL, step, 0)
    low = below((8, 128))
    for b in range(NB):
        a0, a1 = acc[b * 16 : b * 16 + 8, :], acc[b * 16 + 8 : b * 16 + 16, :]
        out, i = outs[b * len(outs) // NB], b % (NB // len(outs))
        out[i * 8 : (i + 1) * 8, :] = jnp.where(
            low, a0 + pltpu.roll(a0, 64, 1), a1 + pltpu.roll(a1, 64, 1)
        )


def product(backward, count, rows, cols, x, w):
    smem = pl.BlockSpec(memory_space=pltpu.SMEM)
    vmem = pl.BlockSpec(memory_space=pltpu.VMEM)
    tables, outs = (1, 2) if backward else (2, 4)
    return pl.pallas_call(
        backward_kernel if backward else forward_kernel,
        in_specs=[smem] * 3 + [vmem] * 2,
        out_specs=[vmem] * outs,
        out_shape=[jax.ShapeDtypeStruct((NB * 8 // outs, 128), jnp.float32)] * outs,
        scratch_shapes=[pltpu.VMEM((NB * NV, 128), jnp.bfloat16)] * tables
        + [pltpu.VMEM((NB * NV, 128), jnp.float32)],
        compiler_params=pltpu.CompilerParams(vmem_limit_bytes=16 * MIB),
        name="backward" if backward else "forward",
    )(count, rows, cols, x, w)


def finish_kernel(a0_ref, a1_ref, b0_ref, b1_ref, o_ref, tmp):
    back = even_odd(jnp.float32)
    tmp[...] = (b0_ref[...] + b1_ref[...]) + lax.dot_general(
        a0_ref[...] + a1_ref[...],
        back,
        (((1,), (1,)), ((), ())),
        preferred_element_type=jnp.float32,
        precision=lax.Precision.HIGHEST,
    )
    for q in range(8):
        o_ref[:, q * 128 : (q + 1) * 128] = tmp[pl.ds(q, 8, stride=8), :]


def finish(a, b):
    vmem = pl.BlockSpec(memory_space=pltpu.VMEM)
    return pl.pallas_call(
        finish_kernel,
        in_specs=[vmem] * 4,
        out_specs=vmem,
        out_shape=jax.ShapeDtypeStruct((8, NV * BS), jnp.float32),
        scratch_shapes=[pltpu.VMEM((64, 128), jnp.float32)],
        compiler_params=pltpu.CompilerParams(vmem_limit_bytes=4 * MIB),
        name="finish",
    )(*a, *b)


def swap(x, axis, bit):
    return lax.ppermute(x, axis, [(s, s ^ (1 << bit)) for s in range(16)])


def gather(x, axis, bits, after=None):
    for k, bit in enumerate(bits):
        y = swap(x, axis, bit)
        if after is not None:
            after.append(y)
        x = jnp.concatenate([x, y], 0)
    return x


def scatter(keep, send, axis, bits):
    for k in reversed(range(len(bits))):
        received = swap(send, axis, bits[k])
        if k == 0:
            return keep, received
        half = keep.shape[0] // 2
        keep, send = keep[:half] + received[:half], keep[half:] + received[half:]


def scatter_by_four(parts, axis, bits):
    masks = [0, 1 << bits[2], 1 << bits[3], (1 << bits[2]) | (1 << bits[3])]
    got = [
        lax.ppermute(parts[k], axis, [(s, s ^ masks[k]) for s in range(16)]) for k in (1, 3, 2)
    ]
    half = parts[0].shape[0] // 2
    keep, send = (
        (parts[0][cut] + got[0][cut]) + (got[1][cut] + got[2][cut])
        for cut in (slice(0, half), slice(half, None))
    )
    return scatter(keep, send, axis, bits[:2])


def place(position, me, bits):
    m = (position >> 3) ^ me
    slot = sum(((m >> bit) & 1) << k for k, bit in enumerate(bits))
    return (slot * 8 + (position & 7)) * 16


def on_device(vectors, block_values, block_rows, block_cols, block_count):
    row_index = lax.axis_index("row")
    col_index = lax.axis_index("col")
    piece = lax.optimization_barrier(vectors.reshape(64, 128))
    got = []
    row_segment = gather(piece, "col", COL_BITS, got)
    if MODE == "a2a":
        copies = jnp.broadcast_to(piece[None], (16, 64, 128))
        column_set = lax.all_to_all(copies, "row", 0, 0, tiled=True).reshape(NB * 8, 128)
    else:
        column_set = gather(piece.reshape(8, 8, 128), "row", ROW_BITS).reshape(NB * 8, 128)
    if "b" in BAR:
        block_rows, block_cols, block_count, _ = lax.optimization_barrier((block_rows, block_cols, block_count, got[0]))
    local_rows = block_rows.reshape(SLOTS)
    local_cols = block_cols.reshape(SLOTS)
    global_row = row_index * NB + local_rows
    global_col = ((local_cols >> 3) * 16 + col_index) * 8 + (local_cols & 7)
    live = jnp.arange(SLOTS, dtype=jnp.int32) < block_count.reshape(())
    weight = jnp.where(live, jnp.where(global_row == global_col, 0.5, 1.0), 0.0)
    weight = jnp.broadcast_to(weight.astype(jnp.float32)[:, None], (SLOTS, 128))
    if "r" in BAR:
        weight, _ = lax.optimization_barrier((weight, got[1]))
    w = relayout(block_values.reshape(SLOTS, BS * BS), weight)
    rows = place(local_rows, col_index, COL_BITS)
    cols = place(local_cols, row_index, ROW_BITS)
    if MODE == "a2a":
        row_part = product(False, block_count, rows, local_cols * 16, column_set, w)
    else:
        row_part = product(False, block_count, rows, cols, column_set, w)
    if "f" in BAR:
        row_segment, _ = lax.optimization_barrier((row_segment, row_part[0]))
    col_part = product(True, block_count, rows, cols, row_segment, w)
    mine_rows = scatter_by_four(row_part, "col", COL_BITS)
    mine_cols = scatter(*col_part, "row", ROW_BITS)
    return finish(mine_rows, mine_cols)


def solution(mesh):
    placed = (
        P(("row", "col"), None),
        P("row", "col", None, None),
        P("row", "col", None),
        P("row", "col", None),
        P("row", "col"),
    )
    return jax.shard_map(
        on_device, mesh=mesh, in_specs=placed, out_specs=P(("row", "col"), None), check_vma=False
    )
```

```python
import functools

import jax
import jax.numpy as jnp
from jax import lax
from jax.experimental import pallas as pl
from jax.experimental.pallas import tpu as pltpu
from jax.sharding import PartitionSpec as P


NV = 16
BS = 64
NB = 128
SLOTS = 512
GROUP = 128
PAD = 33
UNROLL = 64
ROW_BITS = (3, 2, 1, 0)
COL_BITS = (1, 0, 3, 2)
MIB = 1 << 20


def relayout_kernel(v_hbm, weight_ref, w_ref, v_ref, f_ref, sem):
    copies = [
        pltpu.make_async_copy(
            v_hbm.at[pl.ds(i * GROUP, GROUP), :], v_ref.at[pl.ds(i * GROUP, GROUP), :], sem.at[i]
        )
        for i in range(SLOTS // GROUP)
    ]
    for copy in copies:
        copy.start()
    for i, copy in enumerate(copies):
        copy.wait()
        here = slice(i * GROUP, (i + 1) * GROUP)
        weight = weight_ref[here, :]
        for t in range(32):
            x = v_ref[here, t * 128 : (t + 1) * 128].astype(jnp.float32) * weight
            for h in range(GROUP // 8):
                f_ref[pl.ds(h * 8 * PAD + t, 8, stride=PAD), :] = x[h * 8 : (h + 1) * 8]
        for s in range(GROUP):
            to = (i * GROUP + s) * 32
            w_ref[to : to + 32] = f_ref[s * PAD : s * PAD + 32].astype(jnp.bfloat16)


def relayout(values, weight):
    vmem = pl.BlockSpec(memory_space=pltpu.VMEM)
    return pl.pallas_call(
        relayout_kernel,
        in_specs=[pl.BlockSpec(memory_space=pltpu.HBM), vmem],
        out_specs=vmem,
        out_shape=jax.ShapeDtypeStruct((SLOTS * 32, 128), jnp.bfloat16),
        scratch_shapes=[
            pltpu.VMEM((SLOTS, BS * BS), jnp.bfloat16),
            pltpu.VMEM((GROUP * PAD, 128), jnp.float32),
            pltpu.SemaphoreType.DMA((SLOTS // GROUP,)),
        ],
        compiler_params=pltpu.CompilerParams(vmem_limit_bytes=20 * MIB),
        name="relayout",
    )(values, weight)


def even_odd(dtype):
    i = lax.broadcasted_iota(jnp.int32, (128, 128), 0)
    j = lax.broadcasted_iota(jnp.int32, (128, 128), 1)
    k = j % 64
    return (i == (j - k) + 2 * (k % 32) + k // 32).astype(dtype)


def below(shape):
    return lax.broadcasted_iota(jnp.int32, shape, 1) < 64


def offset(ref, s):
    return pl.ds(pl.multiple_of(ref[s], 16), 16)


def pair_of_blocks(w_ref, s):
    w = w_ref[pl.ds(pl.multiple_of(s * 32, 64), 64), :]
    a, b = w[:32], w[32:]
    low = below((32, 128))
    return jnp.concatenate(
        [
            jnp.where(low, a, pltpu.roll(b, 64, 1)),
            jnp.where(low, pltpu.roll(a, 64, 1), b),
        ],
        0,
    )


def to_fixed(totals, out):
    peak = functools.reduce(jnp.maximum, [jnp.abs(total) for total in totals])
    exponent = jnp.floor(jnp.log2(jnp.maximum(peak, 1e-30))) - 14.0
    scale = jnp.exp2(-exponent)
    for i in range(0, len(totals), 2):
        fixed = jnp.concatenate([totals[i] * scale, totals[i + 1] * scale], 0)
        fixed = jnp.clip(jnp.round(fixed), -32767.0, 32767.0)
        out[i * 8 : i * 8 + 16, :] = fixed.astype(jnp.int32).astype(jnp.int16)
    last = len(totals) * 8
    exponent = jnp.concatenate([exponent, exponent], 0)
    out[last : last + 16, :] = exponent.astype(jnp.int32).astype(jnp.int16)


def from_fixed(ref):
    last = ref.shape[0] - 16
    scale = jnp.exp2(ref[last : last + 16, :].astype(jnp.int32).astype(jnp.float32))
    return [
        ref[i : i + 16, :].astype(jnp.int32).astype(jnp.float32) * scale
        for i in range(0, last, 16)
    ]


def combine_kernel(own_ref, *refs):
    *got, keep_ref, send_ref = refs
    pieces = [from_fixed(ref) for ref in got]
    count = own_ref.shape[0] // 16
    totals = []
    for i in range(count):
        total = own_ref[i * 16 : (i + 1) * 16, :]
        for piece in pieces:
            total = total + piece[i]
        if i < count // 2:
            keep_ref[i * 16 : (i + 1) * 16, :] = total
        else:
            totals += [total[:8], total[8:]]
    to_fixed(totals, send_ref)


def combine(own, *got):
    vmem = pl.BlockSpec(memory_space=pltpu.VMEM)
    half = own.shape[0] // 2
    return pl.pallas_call(
        combine_kernel,
        in_specs=[vmem] * (1 + len(got)),
        out_specs=[vmem] * 2,
        out_shape=[
            jax.ShapeDtypeStruct((half, 128), jnp.float32),
            jax.ShapeDtypeStruct((half + 16, 128), jnp.int16),
        ],
        compiler_params=pltpu.CompilerParams(vmem_limit_bytes=4 * MIB),
        name="combine",
    )(own, *got)


def forward_kernel(count_ref, rows_ref, cols_ref, x_ref, w_ref, *outs_and_scratch):
    *outs, xlo, xhi, acc = outs_and_scratch
    low = below((16, 128))
    for b in range(NB // 2):
        x = x_ref[b * 16 : (b + 1) * 16, :].astype(jnp.float32)
        y = pltpu.roll(x, 64, 1)
        for h in range(2):
            here = slice((2 * b + h) * 16, (2 * b + h + 1) * 16)
            p, q = x[h * 8 : (h + 1) * 8], y[h * 8 : (h + 1) * 8]
            zero = jnp.zeros((16, 128), jnp.float32)
            xlo[here, :] = jnp.where(low, jnp.concatenate([p, q], 0), zero).astype(jnp.bfloat16)
            xhi[here, :] = jnp.where(low, zero, jnp.concatenate([q, p], 0)).astype(jnp.bfloat16)
    acc[...] = jnp.zeros_like(acc)

    def step(j, carry):
        for u in range(0, UNROLL, 2):
            s = j * UNROLL + u
            b = pair_of_blocks(w_ref, s)
            x = jnp.concatenate([xlo[offset(cols_ref, s), :], xhi[offset(cols_ref, s + 1), :]], 0)
            f = lax.dot_general(
                x, b, (((1,), (1,)), ((), ())), preferred_element_type=jnp.float32
            )
            acc[offset(rows_ref, s), 0:64] += f[:16]
            acc[offset(rows_ref, s + 1), 0:64] += f[16:]
        return carry

    lax.fori_loop(0, (count_ref[0, 0] + UNROLL - 1) // UNROLL, step, 0)
    low = below((8, 128))
    for part, out in enumerate(outs):
        totals = []
        for b in range(part * NB // 4, (part + 1) * NB // 4):
            a0, a1 = acc[b * 16 : b * 16 + 8, :], acc[b * 16 + 8 : b * 16 + 16, :]
            totals.append(jnp.where(low, a0, pltpu.roll(a1, 64, 1)))
        if part == 0:
            for i, total in enumerate(totals):
                out[i * 8 : (i + 1) * 8, :] = total
        else:
            to_fixed(totals, out)


def backward_kernel(count_ref, rows_ref, cols_ref, x_ref, w_ref, *outs_and_scratch):
    *outs, xs, acc = outs_and_scratch
    order = even_odd(jnp.bfloat16)
    for b in range(NB // 8):
        x = jnp.dot(
            x_ref[b * 64 : (b + 1) * 64, :], order, preferred_element_type=jnp.float32
        )
        y = pltpu.roll(x, 64, 1)
        for h in range(8):
            here = slice((8 * b + h) * 16, (8 * b + h + 1) * 16)
            p, q = x[h * 8 : (h + 1) * 8], y[h * 8 : (h + 1) * 8]
            xs[here, :] = jnp.concatenate([p, q], 0).astype(jnp.bfloat16)
    acc[...] = jnp.zeros_like(acc)

    def step(j, carry):
        for u in range(0, UNROLL, 2):
            s = j * UNROLL + u
            b = pair_of_blocks(w_ref, s)
            x = jnp.concatenate(
                [xs[offset(rows_ref, s), 0:64], xs[offset(rows_ref, s + 1), 0:64]], 0
            )
            g = jnp.dot(x, b, preferred_element_type=jnp.float32)
            acc[offset(cols_ref, s), 0:64] += g[:16, 0:64]
            acc[offset(cols_ref, s + 1), 64:128] += g[16:, 64:128]
        return carry

    lax.fori_loop(0, (count_ref[0, 0] + UNROLL - 1) // UNROLL, step, 0)
    low = below((8, 128))
    for b in range(NB):
        a0, a1 = acc[b * 16 : b * 16 + 8, :], acc[b * 16 + 8 : b * 16 + 16, :]
        out, i = outs[b * len(outs) // NB], b % (NB // len(outs))
        out[i * 8 : (i + 1) * 8, :] = jnp.where(
            low, a0 + pltpu.roll(a0, 64, 1), a1 + pltpu.roll(a1, 64, 1)
        )


def product(backward, count, rows, cols, x, w):
    smem = pl.BlockSpec(memory_space=pltpu.SMEM)
    vmem = pl.BlockSpec(memory_space=pltpu.VMEM)
    if backward:
        tables, outs = 1, 2
        out_shape = [jax.ShapeDtypeStruct((NB * 4, 128), jnp.float32)] * 2
    else:
        tables, outs = 2, 4
        out_shape = [jax.ShapeDtypeStruct((NB * 2, 128), jnp.float32)]
        out_shape += [jax.ShapeDtypeStruct((NB * 2 + 16, 128), jnp.int16)] * 3
    return pl.pallas_call(
        backward_kernel if backward else forward_kernel,
        in_specs=[smem] * 3 + [vmem] * 2,
        out_specs=[vmem] * outs,
        out_shape=out_shape,
        scratch_shapes=[pltpu.VMEM((NB * NV, 128), jnp.bfloat16)] * tables
        + [pltpu.VMEM((NB * NV, 128), jnp.float32)],
        compiler_params=pltpu.CompilerParams(vmem_limit_bytes=16 * MIB),
        name="backward" if backward else "forward",
    )(count, rows, cols, x, w)


def finish_kernel(a0_ref, a1_ref, b0_ref, b1_ref, o_ref, tmp):
    back = even_odd(jnp.float32)
    tmp[...] = (b0_ref[...] + b1_ref[...]) + lax.dot_general(
        a0_ref[...] + jnp.concatenate(from_fixed(a1_ref), 0),
        back,
        (((1,), (1,)), ((), ())),
        preferred_element_type=jnp.float32,
        precision=lax.Precision.HIGHEST,
    )
    for q in range(8):
        o_ref[:, q * 128 : (q + 1) * 128] = tmp[pl.ds(q, 8, stride=8), :]


def finish(a, b):
    vmem = pl.BlockSpec(memory_space=pltpu.VMEM)
    return pl.pallas_call(
        finish_kernel,
        in_specs=[vmem] * 4,
        out_specs=vmem,
        out_shape=jax.ShapeDtypeStruct((8, NV * BS), jnp.float32),
        scratch_shapes=[pltpu.VMEM((64, 128), jnp.float32)],
        compiler_params=pltpu.CompilerParams(vmem_limit_bytes=4 * MIB),
        name="finish",
    )(*a, *b)


def swap(x, axis, mask):
    return lax.ppermute(x, axis, [(s, s ^ mask) for s in range(16)])


def gather(x, axis, bits, after=None):
    for bit in bits:
        y = swap(x, axis, 1 << bit)
        if after is not None:
            after.append(y)
        x = jnp.concatenate([x, y], 0)
    return x


def scatter(keep, send, axis, bits):
    for k in reversed(range(len(bits))):
        received = swap(send, axis, 1 << bits[k])
        if k == 0:
            return keep, received
        half = keep.shape[0] // 2
        keep, send = keep[:half] + received[:half], keep[half:] + received[half:]


def scatter_by_four(parts, axis, bits):
    masks = [0, 1 << bits[2], 1 << bits[3], (1 << bits[2]) | (1 << bits[3])]
    got = [swap(parts[k], axis, masks[k]) for k in (1, 3, 2)]
    keep, send = combine(parts[0], *got)
    keep, send = combine(keep, swap(send, axis, 1 << bits[1]))
    return keep, swap(send, axis, 1 << bits[0])


def place(position, me, bits):
    m = (position >> 3) ^ me
    slot = sum(((m >> bit) & 1) << k for k, bit in enumerate(bits))
    return (slot * 8 + (position & 7)) * 16


def apply(vectors, block_values, block_rows, block_cols, block_count):
    row_index = lax.axis_index("row")
    col_index = lax.axis_index("col")
    piece = lax.optimization_barrier(vectors.reshape(64, 128))
    row_segment = gather(piece, "col", COL_BITS)
    column_set = gather(piece.reshape(8, 8, 128), "row", ROW_BITS).reshape(NB * 8, 128)
    local_rows = block_rows.reshape(SLOTS)
    local_cols = block_cols.reshape(SLOTS)
    rows = place(local_rows, col_index, COL_BITS)
    cols = place(local_cols, row_index, ROW_BITS)
    global_row = row_index * NB + local_rows
    global_col = ((local_cols >> 3) * 16 + col_index) * 8 + (local_cols & 7)
    live = jnp.arange(SLOTS, dtype=jnp.int32) < block_count.reshape(())
    weight = jnp.where(live, jnp.where(global_row == global_col, 0.5, 1.0), 0.0)
    weight = jnp.broadcast_to(weight.astype(jnp.float32)[:, None], (SLOTS, 128))
    values = pltpu.with_memory_space_constraint(block_values.reshape(SLOTS, BS * BS), pltpu.HBM)
    w = relayout(values, weight)
    row_part = product(False, block_count, rows, cols, column_set, w)
    row_segment, _ = lax.optimization_barrier((row_segment, row_part[0]))
    col_part = product(True, block_count, rows, cols, row_segment, w)
    mine_rows = scatter_by_four(row_part, "col", COL_BITS)
    mine_cols = scatter(*col_part, "row", ROW_BITS)
    return finish(mine_rows, mine_cols)


def solution(mesh):
    placed = (
        P(("row", "col"), None),
        P("row", "col", None, None),
        P("row", "col", None),
        P("row", "col", None),
        P("row", "col"),
    )
    return jax.shard_map(
        apply, mesh=mesh, in_specs=placed, out_specs=P(("row", "col"), None), check_vma=False
    )
```

```python
import functools

import jax
import jax.numpy as jnp
from jax import lax
from jax.experimental import pallas as pl
from jax.experimental.pallas import tpu as pltpu
from jax.sharding import PartitionSpec as P


NV = 16
BS = 64
NB = 128
SLOTS = 512
GROUP = 128
PAD = 33
UNROLL = 256
ROW_BITS = (3, 2, 1, 0)
COL_BITS = (1, 0, 3, 2)
MIB = 1 << 20


def relayout_kernel(v_hbm, weight_ref, w_ref, v_ref, f_ref, sem):
    copies = [
        pltpu.make_async_copy(
            v_hbm.at[pl.ds(i * GROUP, GROUP), :], v_ref.at[pl.ds(i * GROUP, GROUP), :], sem.at[i]
        )
        for i in range(SLOTS // GROUP)
    ]
    for copy in copies:
        copy.start()
    for i, copy in enumerate(copies):
        copy.wait()
        here = slice(i * GROUP, (i + 1) * GROUP)
        weight = weight_ref[here, :]
        for t in range(32):
            x = v_ref[here, t * 128 : (t + 1) * 128].astype(jnp.float32) * weight
            for h in range(GROUP // 8):
                f_ref[pl.ds(h * 8 * PAD + t, 8, stride=PAD), :] = x[h * 8 : (h + 1) * 8]
        for s in range(GROUP):
            to = (i * GROUP + s) * 32
            w_ref[to : to + 32] = f_ref[s * PAD : s * PAD + 32].astype(jnp.bfloat16)


def relayout(values, weight):
    vmem = pl.BlockSpec(memory_space=pltpu.VMEM)
    return pl.pallas_call(
        relayout_kernel,
        in_specs=[pl.BlockSpec(memory_space=pltpu.HBM), vmem],
        out_specs=vmem,
        out_shape=jax.ShapeDtypeStruct((SLOTS * 32, 128), jnp.bfloat16),
        scratch_shapes=[
            pltpu.VMEM((SLOTS, BS * BS), jnp.bfloat16),
            pltpu.VMEM((GROUP * PAD, 128), jnp.float32),
            pltpu.SemaphoreType.DMA((SLOTS // GROUP,)),
        ],
        compiler_params=pltpu.CompilerParams(vmem_limit_bytes=20 * MIB),
        name="relayout",
    )(values, weight)


def even_odd(dtype):
    i = lax.broadcasted_iota(jnp.int32, (128, 128), 0)
    j = lax.broadcasted_iota(jnp.int32, (128, 128), 1)
    k = j % 64
    return (i == (j - k) + 2 * (k % 32) + k // 32).astype(dtype)


def below(shape):
    return lax.broadcasted_iota(jnp.int32, shape, 1) < 64


def offset(ref, s):
    return pl.ds(pl.multiple_of(ref[s], 16), 16)


def pair_of_blocks(w_ref, s):
    w = w_ref[pl.ds(pl.multiple_of(s * 32, 64), 64), :]
    a, b = w[:32], w[32:]
    low = below((32, 128))
    return jnp.concatenate(
        [
            jnp.where(low, a, pltpu.roll(b, 64, 1)),
            jnp.where(low, pltpu.roll(a, 64, 1), b),
        ],
        0,
    )


def to_fixed(totals, out):
    peak = functools.reduce(jnp.maximum, [jnp.abs(total) for total in totals])
    exponent = jnp.floor(jnp.log2(jnp.maximum(peak, 1e-30))) - 14.0
    scale = jnp.exp2(-exponent)
    for i in range(0, len(totals), 2):
        fixed = jnp.concatenate([totals[i] * scale, totals[i + 1] * scale], 0)
        fixed = jnp.clip(jnp.round(fixed), -32767.0, 32767.0)
        out[i * 8 : i * 8 + 16, :] = fixed.astype(jnp.int32).astype(jnp.int16)
    last = len(totals) * 8
    exponent = jnp.concatenate([exponent, exponent], 0)
    out[last : last + 16, :] = exponent.astype(jnp.int32).astype(jnp.int16)


def from_fixed(ref):
    if ref.dtype == jnp.float32:
        return [ref[i : i + 16, :] for i in range(0, ref.shape[0], 16)]
    last = ref.shape[0] - 16
    scale = jnp.exp2(ref[last : last + 16, :].astype(jnp.int32).astype(jnp.float32))
    return [
        ref[i : i + 16, :].astype(jnp.int32).astype(jnp.float32) * scale
        for i in range(0, last, 16)
    ]


def combine_kernel(own_ref, *refs):
    *got, keep_ref, send_ref = refs
    pieces = [from_fixed(ref) for ref in got]
    count = own_ref.shape[0] // 16
    totals = []
    for i in range(count):
        total = own_ref[i * 16 : (i + 1) * 16, :]
        for piece in pieces:
            total = total + piece[i]
        if i < count // 2:
            keep_ref[i * 16 : (i + 1) * 16, :] = total
        else:
            totals += [total[:8], total[8:]]
    to_fixed(totals, send_ref)


def combine(own, *got):
    vmem = pl.BlockSpec(memory_space=pltpu.VMEM)
    half = own.shape[0] // 2
    return pl.pallas_call(
        combine_kernel,
        in_specs=[vmem] * (1 + len(got)),
        out_specs=[vmem] * 2,
        out_shape=[
            jax.ShapeDtypeStruct((half, 128), jnp.float32),
            jax.ShapeDtypeStruct((half + 16, 128), jnp.int16),
        ],
        compiler_params=pltpu.CompilerParams(vmem_limit_bytes=4 * MIB),
        name="combine",
    )(own, *got)


def forward_kernel(count_ref, rows_ref, cols_ref, x_ref, w_ref, *outs_and_scratch):
    *outs, xlo, xhi, acc = outs_and_scratch
    low = below((16, 128))
    for b in range(NB // 2):
        x = x_ref[b * 16 : (b + 1) * 16, :].astype(jnp.float32)
        y = pltpu.roll(x, 64, 1)
        for h in range(2):
            here = slice((2 * b + h) * 16, (2 * b + h + 1) * 16)
            p, q = x[h * 8 : (h + 1) * 8], y[h * 8 : (h + 1) * 8]
            zero = jnp.zeros((16, 128), jnp.float32)
            xlo[here, :] = jnp.where(low, jnp.concatenate([p, q], 0), zero).astype(jnp.bfloat16)
            xhi[here, :] = jnp.where(low, zero, jnp.concatenate([q, p], 0)).astype(jnp.bfloat16)
    acc[...] = jnp.zeros_like(acc)

    def step(j, carry):
        for u in range(0, UNROLL, 2):
            s = j * UNROLL + u
            b = pair_of_blocks(w_ref, s)
            x = jnp.concatenate([xlo[offset(cols_ref, s), :], xhi[offset(cols_ref, s + 1), :]], 0)
            f = lax.dot_general(
                x, b, (((1,), (1,)), ((), ())), preferred_element_type=jnp.float32
            )
            acc[offset(rows_ref, s), 0:64] += f[:16]
            acc[offset(rows_ref, s + 1), 0:64] += f[16:]
        return carry

    lax.fori_loop(0, (count_ref[0, 0] + UNROLL - 1) // UNROLL, step, 0)
    low = below((8, 128))
    for part, out in enumerate(outs):
        totals = []
        for b in range(part * NB // 4, (part + 1) * NB // 4):
            a0, a1 = acc[b * 16 : b * 16 + 8, :], acc[b * 16 + 8 : b * 16 + 16, :]
            totals.append(jnp.where(low, a0, pltpu.roll(a1, 64, 1)))
        if part == 0:
            for i, total in enumerate(totals):
                out[i * 8 : (i + 1) * 8, :] = total
        else:
            to_fixed(totals, out)


def backward_kernel(count_ref, rows_ref, cols_ref, x_ref, w_ref, *outs_and_scratch):
    *outs, xs, acc = outs_and_scratch
    order = even_odd(jnp.bfloat16)
    for b in range(NB // 8):
        x = jnp.dot(
            x_ref[b * 64 : (b + 1) * 64, :], order, preferred_element_type=jnp.float32
        )
        y = pltpu.roll(x, 64, 1)
        for h in range(8):
            here = slice((8 * b + h) * 16, (8 * b + h + 1) * 16)
            p, q = x[h * 8 : (h + 1) * 8], y[h * 8 : (h + 1) * 8]
            xs[here, :] = jnp.concatenate([p, q], 0).astype(jnp.bfloat16)
    acc[...] = jnp.zeros_like(acc)

    def step(j, carry):
        for u in range(0, UNROLL, 2):
            s = j * UNROLL + u
            b = pair_of_blocks(w_ref, s)
            x = jnp.concatenate(
                [xs[offset(rows_ref, s), 0:64], xs[offset(rows_ref, s + 1), 0:64]], 0
            )
            g = jnp.dot(x, b, preferred_element_type=jnp.float32)
            acc[offset(cols_ref, s), 0:64] += g[:16, 0:64]
            acc[offset(cols_ref, s + 1), 64:128] += g[16:, 64:128]
        return carry

    lax.fori_loop(0, (count_ref[0, 0] + UNROLL - 1) // UNROLL, step, 0)
    low = below((8, 128))
    for b in range(NB):
        a0, a1 = acc[b * 16 : b * 16 + 8, :], acc[b * 16 + 8 : b * 16 + 16, :]
        out, i = outs[b * len(outs) // NB], b % (NB // len(outs))
        out[i * 8 : (i + 1) * 8, :] = jnp.where(
            low, a0 + pltpu.roll(a0, 64, 1), a1 + pltpu.roll(a1, 64, 1)
        )


def product(backward, count, rows, cols, x, w):
    smem = pl.BlockSpec(memory_space=pltpu.SMEM)
    vmem = pl.BlockSpec(memory_space=pltpu.VMEM)
    if backward:
        tables, outs = 1, 2
        out_shape = [jax.ShapeDtypeStruct((NB * 4, 128), jnp.float32)] * 2
    else:
        tables, outs = 2, 4
        out_shape = [jax.ShapeDtypeStruct((NB * 2, 128), jnp.float32)]
        out_shape += [jax.ShapeDtypeStruct((NB * 2 + 16, 128), jnp.int16)] * 3
    return pl.pallas_call(
        backward_kernel if backward else forward_kernel,
        in_specs=[smem] * 3 + [vmem] * 2,
        out_specs=[vmem] * outs,
        out_shape=out_shape,
        scratch_shapes=[pltpu.VMEM((NB * NV, 128), jnp.bfloat16)] * tables
        + [pltpu.VMEM((NB * NV, 128), jnp.float32)],
        compiler_params=pltpu.CompilerParams(vmem_limit_bytes=16 * MIB),
        name="backward" if backward else "forward",
    )(count, rows, cols, x, w)


def finish_kernel(a0_ref, a1_ref, b0_ref, b1_ref, o_ref, tmp):
    back = even_odd(jnp.float32)
    tmp[...] = (b0_ref[...] + jnp.concatenate(from_fixed(b1_ref), 0)) + lax.dot_general(
        a0_ref[...] + jnp.concatenate(from_fixed(a1_ref), 0),
        back,
        (((1,), (1,)), ((), ())),
        preferred_element_type=jnp.float32,
        precision=lax.Precision.HIGHEST,
    )
    for q in range(8):
        o_ref[:, q * 128 : (q + 1) * 128] = tmp[pl.ds(q, 8, stride=8), :]


def finish(a, b):
    vmem = pl.BlockSpec(memory_space=pltpu.VMEM)
    return pl.pallas_call(
        finish_kernel,
        in_specs=[vmem] * 4,
        out_specs=vmem,
        out_shape=jax.ShapeDtypeStruct((8, NV * BS), jnp.float32),
        scratch_shapes=[pltpu.VMEM((64, 128), jnp.float32)],
        compiler_params=pltpu.CompilerParams(vmem_limit_bytes=4 * MIB),
        name="finish",
    )(*a, *b)


def swap(x, axis, mask):
    return lax.ppermute(x, axis, [(s, s ^ mask) for s in range(16)])


def gather(x, axis, bits, after=None):
    for bit in bits:
        y = swap(x, axis, 1 << bit)
        if after is not None:
            after.append(y)
        x = jnp.concatenate([x, y], 0)
    return x


def scatter(keep, send, axis, bits):
    for k in reversed(range(4)):
        received = swap(send, axis, 1 << bits[k])
        if k == 0:
            return keep, received
        keep, send = combine(keep, received)


def scatter_by_four(parts, axis, bits):
    masks = [0, 1 << bits[2], 1 << bits[3], (1 << bits[2]) | (1 << bits[3])]
    got = [swap(parts[k], axis, masks[k]) for k in (1, 3, 2)]
    keep, send = combine(parts[0], *got)
    keep, send = combine(keep, swap(send, axis, 1 << bits[1]))
    return keep, swap(send, axis, 1 << bits[0])


def place(position, me, bits):
    m = (position >> 3) ^ me
    slot = sum(((m >> bit) & 1) << k for k, bit in enumerate(bits))
    return (slot * 8 + (position & 7)) * 16


def apply(vectors, block_values, block_rows, block_cols, block_count):
    row_index = lax.axis_index("row")
    col_index = lax.axis_index("col")
    piece = lax.optimization_barrier(vectors.reshape(64, 128))
    row_segment = gather(piece, "col", COL_BITS)
    column_set = gather(piece.reshape(8, 8, 128), "row", ROW_BITS).reshape(NB * 8, 128)
    local_rows = block_rows.reshape(SLOTS)
    local_cols = block_cols.reshape(SLOTS)
    rows = place(local_rows, col_index, COL_BITS)
    cols = place(local_cols, row_index, ROW_BITS)
    global_row = row_index * NB + local_rows
    global_col = ((local_cols >> 3) * 16 + col_index) * 8 + (local_cols & 7)
    live = jnp.arange(SLOTS, dtype=jnp.int32) < block_count.reshape(())
    weight = jnp.where(live, jnp.where(global_row == global_col, 0.5, 1.0), 0.0)
    weight = jnp.broadcast_to(weight.astype(jnp.float32)[:, None], (SLOTS, 128))
    values = pltpu.with_memory_space_constraint(block_values.reshape(SLOTS, BS * BS), pltpu.HBM)
    w = relayout(values, weight)
    row_part = product(False, block_count, rows, cols, column_set, w)
    row_segment, _ = lax.optimization_barrier((row_segment, row_part[0]))
    col_part = product(True, block_count, rows, cols, row_segment, w)
    mine_rows = scatter_by_four(row_part, "col", COL_BITS)
    mine_cols = scatter(*col_part, "row", ROW_BITS)
    return finish(mine_rows, mine_cols)


def solution(mesh):
    placed = (
        P(("row", "col"), None),
        P("row", "col", None, None),
        P("row", "col", None),
        P("row", "col", None),
        P("row", "col"),
    )
    return jax.shard_map(
        apply, mesh=mesh, in_specs=placed, out_specs=P(("row", "col"), None), check_vma=False
    )
```
